32 devices in a mesh: layer: 2 (over core), feat: 4 (over y, x), seq: 4 (over z).
Axes of the slice: x: 2, y: 2, z: 4, core: 2. Of those that a mesh axis runs over, the one named last changes fastest.
Arguments:
- mlp_inputs: bfloat16 [2, 768, 2304], P('layer', 'seq'), may hold values from -6 to 6
- enc_weight: bfloat16 [2, 2304, 4096], P('layer', 'seq', 'feat'), may hold values from -0.125 to 0.125
- enc_bias: float32 [2, 4096], P('layer', 'feat'), may hold values from -3 to 3
- dec_weight: bfloat16 [2, 4096, 2304], P('layer', 'feat', 'seq'), may hold values from -0.1875 to 0.1875
- dec_cross: bfloat16 [4096, 2304], P('feat', ('layer', 'seq')), may hold values from -0.1875 to 0.1875
- dec_bias: float32 [2, 2304], P('layer', 'feat'), may hold values from -3 to 3
Outputs:
- recon: bfloat16 [2, 768, 2304], P('layer', 'seq', 'feat')
The draws below stay inside these ranges and needn't reach their ends.
All inputs are finite; a program needn't handle non-finite values.
Results may differ from the reference program's by a relative error of at most 0.0047.
Values may be sent and summed in bfloat16 or wider, within the bound.
A program may use at most 64 MiB of HBM per device.

```python
import jax
import jax.numpy as jnp

D = 2304
F = 4096
TOKENS = 768


def spiked(result, own_key, source, target, blocks, factor):
    owner, partner = [(jnp.arange(result.shape[dim]) // (result.shape[dim] // blocks)).reshape([-1 if axis == dim else 1 for axis in range(result.ndim)]) for dim in (source, target)]
    chosen = jax.random.permutation(own_key, blocks)[partner]
    strong = (owner == chosen) | (owner == (partner + blocks // 2) % blocks)
    return jnp.where(strong, factor * result, result)


def level_of(own_key, shape, cuts, smallest, largest):
    loudness, own = 1.0, jax.random.fold_in(own_key, 6)
    for dim, parts in cuts:
        steps = jnp.exp(jax.random.uniform(jax.random.fold_in(own, dim), (parts,), jnp.float32, smallest / len(cuts), largest / len(cuts)))
        loudness = loudness * jnp.repeat(steps, shape[dim] // parts).reshape([-1 if axis == dim else 1 for axis in range(len(shape))])
    return loudness


def noise(key, dims, deviation, limit, pieces=(), kind=jnp.bfloat16):
    values = jax.random.normal(key, dims, jnp.float32) * deviation
    if len(pieces) > 0:
        values = level_of(key, dims, pieces, -0.22, 0.18) * values
    return jnp.clip(values, min=-limit, max=limit).astype(kind)


def noise_with(own_key, shape, scale, reach, split, heavy, dtype=jnp.bfloat16):
    entries = scale * jax.random.normal(own_key, shape, jnp.float32)
    if split:
        entries = entries * level_of(own_key, shape, split, -0.22, 0.18)
    return jnp.clip(spiked(entries, jax.random.fold_in(own_key, 3), *heavy), -reach, reach).astype(dtype)


def setup_inputs(seed: int = 0) -> dict:
    key_of = jax.random.split(jax.random.key(seed), 7)
    return {
        "mlp_inputs": noise(key_of[0], (2, TOKENS, D), 1.0, 6.0, ((0, 2), (1, 4))),
        "enc_weight": noise(key_of[1], (2, D, F), D ** -0.5, 0.125, ((0, 2), (1, 4), (2, 4))),
        "enc_bias": noise(key_of[2], (2, F), 0.5, 3.0, ((0, 2), (1, 4)), jnp.float32),
        "dec_weight": noise_with(key_of[3], (2, F, D), (F // 2) ** -0.5, 0.1875, ((0, 2), (1, 4), (2, 4)), (1, 2, 4, 2.0)),
        "dec_cross": noise_with(key_of[4], (F, D), (F // 2) ** -0.5, 0.1875, ((0, 4), (1, 8)), (0, 1, 8, 2.0)),
        "dec_bias": noise(key_of[5], (2, D), 0.5, 3.0, ((0, 2), (1, 4)), jnp.float32),
    }


def reference(mlp_inputs, enc_weight, enc_bias, dec_weight, dec_cross, dec_bias):
    first = jnp.dot(mlp_inputs[0], enc_weight[0], preferred_element_type=jnp.float32) + enc_bias[0]
    first = jnp.maximum(first, 0.0).astype(jnp.bfloat16)
    second = jnp.dot(mlp_inputs[1], enc_weight[1], preferred_element_type=jnp.float32) + enc_bias[1]
    second = jnp.maximum(second, 0.0).astype(jnp.bfloat16)
    own_first = jnp.dot(first, dec_weight[0], preferred_element_type=jnp.float32)
    own_second = jnp.dot(second, dec_weight[1], preferred_element_type=jnp.float32)
    cross_terms = jnp.dot(first, dec_cross, preferred_element_type=jnp.float32)
    recon_first = (own_first + dec_bias[0]).astype(jnp.bfloat16)
    recon_second = (own_second + cross_terms + dec_bias[1]).astype(jnp.bfloat16)
    return jnp.stack([recon_first, recon_second], axis=0)
```

```python
import functools

import jax
import jax.numpy as jnp
from jax import lax
from jax.experimental import pallas as pl
from jax.experimental.pallas import tpu as pltpu
from jax.sharding import PartitionSpec as P

MESH = pl.DeviceIdType.MESH
F32, BF16 = jnp.float32, jnp.bfloat16


def passed_along(x, axis, by):
    devices = lax.axis_size(axis)
    pairs = [(i, i + by) for i in range(devices) if 0 <= i + by < devices]
    return lax.ppermute(x, axis, pairs)


def per_device(mlp_inputs, enc_weight, enc_bias, dec_weight, dec_cross, dec_bias):
    token_rows = mlp_inputs[0]
    layer_index = lax.axis_index("layer")
    pre_acts = jnp.dot(
        token_rows,
        lax.all_gather(enc_weight[0], "seq", axis=0, tiled=True),
        preferred_element_type=F32,
    )
    features = jnp.maximum(pre_acts + enc_bias[0], 0.0).astype(BF16)
    own_terms = jnp.dot(
        features,
        lax.all_gather(dec_weight[0], "seq", axis=1, tiled=True),
        preferred_element_type=F32,
    )
    half_rows = features.shape[0] // 2
    sent_half = passed_along(features[half_rows:], "layer", 1)
    cross_input = jnp.where(layer_index == 0, features[:half_rows], sent_half)
    cross_terms = jnp.dot(
        cross_input,
        lax.all_gather(dec_cross, ("layer", "seq"), axis=1, tiled=True),
        preferred_element_type=F32,
    )
    own_sums, cross_sums = (
        lax.psum_scatter(own_terms, "feat", scatter_dimension=1, tiled=True),
        lax.psum_scatter(cross_terms, "feat", scatter_dimension=1, tiled=True),
    )
    moved_sums = passed_along(cross_sums, "layer", 1)
    cross_full = jnp.concatenate([moved_sums, cross_sums], axis=0)
    total = own_sums + dec_bias[0] + jnp.where(layer_index == 1, cross_full, 0.0)
    return total.astype(BF16)[None]


def kernel(
    n, x_ref, enc_ref, encb_ref, dec_hbm, cross_hbm, decb_ref, out_ref,
    dec_ref, cross_ref, cross2_ref, xsend, xall, pf, rs_send, rs_up, rs_dn, feats,
    oown, osend, orecv, csend, crecv, rsum, ztr, crs, zcr, fin, fcr,
    ld_sem, cw_s, cw_r, x1_s, x1_r, x2_s, x2_r, rs_s, ru_r, rd_r, au_s, au_r, ad_s, ad_r,
    o_s, o_r, c_s, c_r, e_s, e_r, ec_s, ec_r, f_s, f_r, fc_s, fc_r,
):
    layer, f, z = lax.axis_index("layer"), lax.axis_index("feat"), lax.axis_index("seq")
    r = x_ref.shape[0] // n
    k = enc_ref.shape[0]
    half = cross_ref.shape[1]
    first, second = layer == 0, layer == 1
    order = list(range(1, n)) + [0]

    def peer(dx):
        return lax.rem(f + dx, n)

    def rows(t):
        return pl.ds(pl.multiple_of(t * r, r), r)

    pending = []

    def copy(src, dst, ss, rs, to):
        a, b, c = to
        return pltpu.make_async_remote_copy(
            src_ref=src, dst_ref=dst, send_sem=ss, recv_sem=rs,
            device_id={"layer": a, "feat": b, "seq": c}, device_id_type=MESH,
        )

    def send(cond, make):
        if cond is None:
            make().start()
        else:
            pl.when(cond)(lambda: make().start())
        pending.append((cond, make))

    def arrive(cond, dst, sem):
        def wait():
            copy(dst, dst, sem, sem, (layer, f, z)).wait_recv()
        if cond is None:
            wait()
        else:
            pl.when(cond)(wait)

    load_dec = pltpu.make_async_copy(dec_hbm, dec_ref, ld_sem.at[0])
    load_dec.start()
    load_cross = pltpu.make_async_copy(cross_hbm, cross_ref, ld_sem.at[1])
    load_cross.start()

    barrier = pltpu.get_barrier_semaphore()
    greeted = [(layer, f, lax.rem(z + d, n)) for d in range(1, n)]
    greeted += [(layer, peer(d), z) for d in range(1, n)]
    greeted += [(1 - layer, peer(d), z) for d in range(n)]
    for a, b, c in greeted:
        pl.semaphore_signal(
            barrier, inc=1, device_id={"layer": a, "feat": b, "seq": c}, device_id_type=MESH
        )

    for t in range(n):
        xsend[t] = x_ref[rows(f), t * k:(t + 1) * k]
    pl.semaphore_wait(barrier, len(greeted))
    for d in range(n - 1, 0, -1):
        for sign in (1, -1):
            t = z + sign * d
            send(
                (t < n) & (t >= 0),
                lambda t=t, d=d, sign=sign: copy(
                    xsend.at[t], xall.at[f, rows(z)], x1_s.at[t], x1_r.at[z], (layer, f, t)
                ),
            )
    for t in range(n):
        @pl.when(t == z)
        def _(t=t):
            for p in range(n):
                xall[p, t * r:(t + 1) * r] = x_ref[p * r:(p + 1) * r, t * k:(t + 1) * k]
    load_cross.wait()
    send(second, lambda: copy(cross_ref, cross2_ref, cw_s.at[0], cw_r.at[0], (0, f, z)))
    for d in range(1, n):
        for sign in (1, -1):
            t = z + sign * d
            ok = (t < n) & (t >= 0)

            def wait(t=t):
                arrive(None, xall.at[f, rows(t)], x1_r.at[t])
            pl.when(ok)(wait)
            for dx in range(1, n):
                send(
                    ok,
                    lambda t=t, dx=dx: copy(
                        xall.at[f, rows(t)], xall.at[f, rows(t)],
                        x2_s.at[dx, t], x2_r.at[dx, t], (layer, peer(dx), z)
                    ),
                )

    def stage_a(i):
        dx = order[i]
        p = peer(dx)
        if dx:
            for t in range(n):
                arrive(t != z, xall.at[p, rows(t)], x2_r.at[n - dx, t])
        pf[i] = jnp.dot(xall[p], enc_ref[...], preferred_element_type=F32)
        for t in range(n - 1, 0, -1):
            @pl.when(z == 0)
            def _(t=t):
                rs_send[i, t * r:(t + 1) * r] = pf[i, t * r:(t + 1) * r].astype(BF16)
            send(z == 0, lambda t=t: copy(
                rs_send.at[i, pl.ds(t * r, r)], rs_up.at[i, pl.ds(t * r, r)],
                rs_s.at[i, t], ru_r.at[i, t], (layer, f, z + 1)))
        for t in range(n - 1):
            @pl.when(z == n - 1)
            def _(t=t):
                rs_send[i, t * r:(t + 1) * r] = pf[i, t * r:(t + 1) * r].astype(BF16)
            send(z == n - 1, lambda t=t: copy(
                rs_send.at[i, pl.ds(t * r, r)], rs_dn.at[i, pl.ds(t * r, r)],
                rs_s.at[i, t], rd_r.at[i, t], (layer, f, z - 1)))

    def relay_up(i, t):
        ok = (z > 0) & (z < t)
        part = pl.ds(t * r, r)

        @pl.when(ok)
        def _():
            arrive(None, rs_up.at[i, part], ru_r.at[i, t])
            rs_send[i, part] = (pf[i, part] + rs_up[i, part].astype(F32)).astype(BF16)
        send(ok, lambda: copy(
            rs_send.at[i, part], rs_up.at[i, part], rs_s.at[i, t], ru_r.at[i, t], (layer, f, z + 1)))

    def relay_down(i, t):
        ok = (z < n - 1) & (z > t)
        part = pl.ds(t * r, r)

        @pl.when(ok)
        def _():
            arrive(None, rs_dn.at[i, part], rd_r.at[i, t])
            rs_send[i, part] = (pf[i, part] + rs_dn[i, part].astype(F32)).astype(BF16)
        send(ok, lambda: copy(
            rs_send.at[i, part], rs_dn.at[i, part], rs_s.at[i, t], rd_r.at[i, t], (layer, f, z - 1)))

    def stage_b(i):
        for s in range(n - 1):
            relay_up(i, n - 1 - s)
            relay_down(i, s)
        mine = rows(z)

        @pl.when(z > 0)
        def _():
            arrive(None, rs_up.at[i, mine], ru_r.at[i, z])
            pf[i, mine] = pf[i, mine] + rs_up[i, mine].astype(F32)

        @pl.when(z < n - 1)
        def _():
            arrive(None, rs_dn.at[i, mine], rd_r.at[i, z])
            pf[i, mine] = pf[i, mine] + rs_dn[i, mine].astype(F32)
        feats[i, mine] = jnp.maximum(pf[i, mine] + encb_ref[...], 0.0).astype(BF16)
        send(z < n - 1, lambda: copy(
            feats.at[i, mine], feats.at[i, mine], au_s.at[i, z], au_r.at[i, z], (layer, f, z + 1)))
        send(z > 0, lambda: copy(
            feats.at[i, mine], feats.at[i, mine], ad_s.at[i, z], ad_r.at[i, z], (layer, f, z - 1)))

    def stage_c(i):
        for d in range(1, n):
            for sign, ss, rr in ((-1, au_s, au_r), (1, ad_s, ad_r)):
                t = z + sign * d
                ok = (t >= 0) & (t < n)

                def wait(t=t, rr=rr):
                    arrive(None, feats.at[i, rows(t)], rr.at[i, t])
                pl.when(ok)(wait)
                further = ok & ((z < n - 1) if sign < 0 else (z > 0))
                send(further, lambda t=t, ss=ss, rr=rr, sign=sign: copy(
                    feats.at[i, rows(t)], feats.at[i, rows(t)], ss.at[i, t], rr.at[i, t],
                    (layer, f, z - sign)))

    def stage_d(i):
        dx = order[i]
        terms = jnp.dot(feats[i], dec_ref[...], preferred_element_type=F32)
        if dx:
            osend[dx] = terms.astype(BF16)
            send(None, lambda: copy(
                osend.at[dx], orecv.at[dx], o_s.at[dx], o_r.at[dx], (layer, peer(dx), z)))
        else:
            oown[...] = terms

        @pl.when(first)
        def _():
            a = jnp.dot(feats[i], cross_ref[...], preferred_element_type=F32)
            b = jnp.dot(feats[i], cross2_ref[...], preferred_element_type=F32)
            csend[dx] = jnp.concatenate([a, b], axis=1).astype(BF16)
        send(first, lambda: copy(
            csend.at[dx], crecv.at[dx], c_s.at[dx], c_r.at[dx], (1, peer(dx), z)))

    stage_a(0)
    for i in range(n):
        if i + 1 < n:
            stage_a(i + 1)
        stage_b(i)
        if i == 0:
            load_dec.wait()
            arrive(first, cross2_ref, cw_r.at[0])
        else:
            stage_c(i - 1)
            stage_d(i - 1)
    stage_c(n - 1)
    stage_d(n - 1)

    for dx in range(1, n):
        arrive(None, orecv.at[dx], o_r.at[dx])
        oown[...] += orecv[dx].astype(F32)
    for t in range(n):
        rsum[t] = oown[t * r:(t + 1) * r].astype(BF16)

    def scatter(cond, src, dst, ss, rs, t):
        send(cond, lambda: copy(src.at[t], dst.at[z], ss.at[t], rs.at[z], (layer, f, t)))

    for t in range(n):
        scatter(t != z, rsum, ztr, e_s, e_r, t)
    for dx in range(n):
        arrive(second, crecv.at[dx], c_r.at[dx])

    @pl.when(second)
    def _():
        sums = crecv[0].astype(F32)
        for dx in range(1, n):
            sums += crecv[dx].astype(F32)
        for t in range(n):
            for h in range(2):
                crs[h, t] = sums[t * r:(t + 1) * r, h * half:(h + 1) * half].astype(BF16)
    for t in range(n):
        for h in range(2):
            scatter(second & (t != z), crs.at[h], zcr.at[h], ec_s.at[h], ec_r.at[h], t)
    ztr[z] = rsum[z]

    @pl.when(second)
    def _():
        for h in range(2):
            zcr[h, z] = crs[h, z]

    for t in range(n):
        arrive(t != z, ztr.at[t], e_r.at[t])

        @pl.when(t == f)
        def _(t=t):
            fin[f] = ztr[t]
        send(t != f, lambda t=t: copy(
            ztr.at[t], fin.at[f], f_s.at[t], f_r.at[f], (layer, t, z)))
    for t in range(n):
        for h in range(2):
            arrive(second & (t != z), zcr.at[h, t], ec_r.at[h, t])
            to, j = (h * n + t) // 2, (h * n + t) % 2

            @pl.when(second & (to == f))
            def _(t=t, h=h, j=j):
                fcr[j, f] = zcr[h, t]
            send(second & (to != f), lambda t=t, h=h, to=to, j=j: copy(
                zcr.at[h, t], fcr.at[j, f], fc_s.at[h, t], fc_r.at[j, f], (layer, to, z)))
    for g in range(n):
        arrive(g != f, fin.at[g], f_r.at[g])
        for j in range(2):
            arrive(second & (g != f), fcr.at[j, g], fc_r.at[j, g])
        part = slice(g * r, (g + 1) * r)

        @pl.when(first)
        def _(g=g, part=part):
            out_ref[part] = (fin[g].astype(F32) + decb_ref[...]).astype(BF16)

        @pl.when(second)
        def _(g=g, part=part):
            cross = jnp.concatenate([fcr[0, g].astype(F32), fcr[1, g].astype(F32)], axis=1)
            out_ref[part] = (fin[g].astype(F32) + cross + decb_ref[...]).astype(BF16)

    for cond, make in pending:
        if cond is None:
            make().wait_send()
        else:
            pl.when(cond)(lambda make=make: make().wait_send())


def by_kernel(n, mlp_inputs, enc_weight, enc_bias, dec_weight, dec_cross, dec_bias):
    x, enc, dec = mlp_inputs[0], enc_weight[0], dec_weight[0]
    r = x.shape[0] // n
    k, wide = enc.shape
    cols, half = dec.shape[1], dec_cross.shape[1]
    vmem = pl.BlockSpec(memory_space=pltpu.VMEM)
    hbm = pl.BlockSpec(memory_space=pl.ANY)
    dma = pltpu.SemaphoreType.DMA
    every = n * r
    scratch = [
        pltpu.VMEM(dec.shape, BF16),
        pltpu.VMEM(dec_cross.shape, BF16),
        pltpu.VMEM(dec_cross.shape, BF16),
        pltpu.VMEM((n, r, k), BF16),
        pltpu.VMEM((n, every, k), BF16),
        pltpu.VMEM((n, every, wide), F32),
        pltpu.VMEM((n, every, wide), BF16),
        pltpu.VMEM((n, every, wide), BF16),
        pltpu.VMEM((n, every, wide), BF16),
        pltpu.VMEM((n, every, wide), BF16),
        pltpu.VMEM((every, cols), F32),
        pltpu.VMEM((n, every, cols), BF16),
        pltpu.VMEM((n, every, cols), BF16),
        pltpu.VMEM((n, every, 2 * half), BF16),
        pltpu.VMEM((n, every, 2 * half), BF16),
        pltpu.VMEM((n, r, cols), BF16),
        pltpu.VMEM((n, r, cols), BF16),
        pltpu.VMEM((2, n, r, half), BF16),
        pltpu.VMEM((2, n, r, half), BF16),
        pltpu.VMEM((n, r, cols), BF16),
        pltpu.VMEM((2, n, r, half), BF16),
        dma((2,)), dma((1,)), dma((1,)),
        dma((n,)), dma((n,)), dma((n, n)), dma((n, n)),
        dma((n, n)), dma((n, n)), dma((n, n)),
        dma((n, n)), dma((n, n)), dma((n, n)), dma((n, n)),
        dma((n,)), dma((n,)), dma((n,)), dma((n,)),
        dma((n,)), dma((n,)), dma((2, n)), dma((2, n)),
        dma((n,)), dma((n,)), dma((2, n)), dma((2, n)),
    ]
    out = pl.pallas_call(
        functools.partial(kernel, n),
        out_shape=jax.ShapeDtypeStruct((x.shape[0], cols), BF16),
        in_specs=[vmem, vmem, vmem, hbm, hbm, vmem],
        out_specs=vmem,
        scratch_shapes=scratch,
        compiler_params=pltpu.CompilerParams(
            collective_id=0, has_side_effects=True, vmem_limit_bytes=56 * 2**20
        ),
    )(x, enc, enc_bias, dec, dec_cross, dec_bias)
    return out[None]


def solution(mesh):
    placed = (
        P("layer", "seq", None),
        P("layer", "seq", "feat"),
        P("layer", "feat"),
        P("layer", "feat", "seq"),
        P("feat", ("layer", "seq")),
        P("layer", "feat"),
    )
    groups = mesh.shape["feat"]

    def body(mlp_inputs, *rest):
        fits = groups == mesh.shape["seq"] and mlp_inputs.shape[1] % (16 * groups) == 0
        if fits and mesh.shape["layer"] == 2 and groups % 2 == 0:
            return by_kernel(groups, mlp_inputs, *rest)
        return per_device(mlp_inputs, *rest)

    return jax.shard_map(
        body, mesh=mesh, in_specs=placed, out_specs=P("layer", "seq", "feat"), check_vma=False
    )
```

```python
import functools
import heapq

import jax
import jax.numpy as jnp
from jax import lax
from jax.experimental import pallas as pl
from jax.experimental.pallas import tpu as pltpu
from jax.sharding import PartitionSpec as P

MESH = pl.DeviceIdType.MESH
F32, BF16 = jnp.float32, jnp.bfloat16


def passed_along(x, axis, by):
    devices = lax.axis_size(axis)
    pairs = [(i, i + by) for i in range(devices) if 0 <= i + by < devices]
    return lax.ppermute(x, axis, pairs)


def per_device(mlp_inputs, enc_weight, enc_bias, dec_weight, dec_cross, dec_bias):
    token_rows = mlp_inputs[0]
    layer_index = lax.axis_index("layer")
    pre_acts = jnp.dot(
        token_rows,
        lax.all_gather(enc_weight[0], "seq", axis=0, tiled=True),
        preferred_element_type=F32,
    )
    features = jnp.maximum(pre_acts + enc_bias[0], 0.0).astype(BF16)
    own_terms = jnp.dot(
        features,
        lax.all_gather(dec_weight[0], "seq", axis=1, tiled=True),
        preferred_element_type=F32,
    )
    half_rows = features.shape[0] // 2
    sent_half = passed_along(features[half_rows:], "layer", 1)
    cross_input = jnp.where(layer_index == 0, features[:half_rows], sent_half)
    cross_terms = jnp.dot(
        cross_input,
        lax.all_gather(dec_cross, ("layer", "seq"), axis=1, tiled=True),
        preferred_element_type=F32,
    )
    own_sums, cross_sums = (
        lax.psum_scatter(own_terms, "feat", scatter_dimension=1, tiled=True),
        lax.psum_scatter(cross_terms, "feat", scatter_dimension=1, tiled=True),
    )
    moved_sums = passed_along(cross_sums, "layer", 1)
    cross_full = jnp.concatenate([moved_sums, cross_sums], axis=0)
    total = own_sums + dec_bias[0] + jnp.where(layer_index == 1, cross_full, 0.0)
    return total.astype(BF16)[None]

ROW_CUTS, COL_CUTS = 3, 1


def plan_line(n, steps, per_piece, piece=2.1, lag=1.7, touch=0.1):
    wire = piece / per_piece

    def run(ahead):
        link, free = {}, [0.0] * n
        got, todo, heap, lists = {}, {}, [], [[] for _ in range(n)]
        serial = [0]

        def post(now, z, to, msg):
            start = max(link.get((z, to), 0.0), now)
            link[z, to] = start + wire
            serial[0] += 1
            heapq.heappush(heap, (start + wire + lag, serial[0], to, msg))

        def start(now, z, s):
            if s < steps and z in (0, n - 1):
                lists[z].append(("init", s, 0, 0))
                for t in range(n - 1, 0, -1) if z == 0 else range(n - 1):
                    post(now, z, 1 if z == 0 else n - 2, ("rs", s, t, 1 if z == 0 else -1))

        def finish(z, s):
            key = (z, s // per_piece)
            todo[key] = todo.get(key, 0) + 1
            if todo[key] == per_piece * n:
                lists[z].append(("piece", s // per_piece, 0, 0))

        for s in range(ahead):
            for z in (0, n - 1):
                start(0.0, z, s)
        while heap:
            now, _, z, (kind, s, t, way) = heapq.heappop(heap)
            now = max(now, free[z]) + touch
            free[z] = now
            if kind == "rs" and t != z:
                lists[z].append(("relay", s, t, way))
                post(now, z, z + way, (kind, s, t, way))
            elif kind == "rs":
                got[z, s] = got.get((z, s), 0) + 1
                if got[z, s] == (z > 0) + (z < n - 1):
                    lists[z].append(("own", s, 0, 0))
                    for to in (z + 1, z - 1):
                        if 0 <= to < n:
                            post(now, z, to, ("ag", s, z, to - z))
                    start(now, z, s + ahead)
                    finish(z, s)
            else:
                lists[z].append(("ag", s, t, way))
                if 0 <= z + way < n:
                    post(now, z, z + way, (kind, s, t, way))
                finish(z, s)
        return max(free), ahead, lists

    return min(run(ahead) for ahead in range(1, steps + 1))


def kernel(
    n, x_ref, enc_ref, encb_ref, dec_hbm, cross_hbm, decb_ref, out_ref,
    dec_ref, cross_ref, cross2_ref, xsend, xall, pf, rs_send, rs_up, rs_dn, feats,
    oown, osend, orecv, csend, crecv, rsum, ztr, crs, zcr, fin, fcr,
    ld_sem, cw_s, cw_r, x1_s, x1_r, x2_s, x2_r, rs_s, ru_r, rd_r, au_s, au_r, ad_s, ad_r,
    o_s, o_r, c_s, c_r, e_s, e_r, ec_s, ec_r, f_s, f_r, fc_s, fc_r,
):
    layer, f, z = lax.axis_index("layer"), lax.axis_index("feat"), lax.axis_index("seq")
    r = x_ref.shape[0] // n
    k = enc_ref.shape[0]
    half = cross_ref.shape[1]
    first, second = layer == 0, layer == 1
    order = list(range(1, n)) + [0]

    def peer(dx):
        return lax.rem(f + dx, n)

    def rows(t):
        return pl.ds(pl.multiple_of(t * r, r), r)

    pending = []

    def copy(src, dst, ss, rs, to):
        a, b, c = to
        return pltpu.make_async_remote_copy(
            src_ref=src, dst_ref=dst, send_sem=ss, recv_sem=rs,
            device_id={"layer": a, "feat": b, "seq": c}, device_id_type=MESH,
        )

    def send(cond, make):
        if cond is None:
            make().start()
        else:
            pl.when(cond)(lambda: make().start())
        pending.append((cond, make))

    def arrive(cond, dst, sem):
        def wait():
            copy(dst, dst, sem, sem, (layer, f, z)).wait_recv()
        if cond is None:
            wait()
        else:
            pl.when(cond)(wait)

    load_dec = pltpu.make_async_copy(dec_hbm, dec_ref, ld_sem.at[0])
    load_dec.start()
    load_cross = pltpu.make_async_copy(cross_hbm, cross_ref, ld_sem.at[1])
    load_cross.start()

    barrier = pltpu.get_barrier_semaphore()
    greeted = [(layer, f, lax.rem(z + d, n)) for d in range(1, n)]
    greeted += [(layer, peer(d), z) for d in range(1, n)]
    greeted += [(1 - layer, peer(d), z) for d in range(n)]
    for a, b, c in greeted:
        pl.semaphore_signal(
            barrier, inc=1, device_id={"layer": a, "feat": b, "seq": c}, device_id_type=MESH
        )

    for t in range(n):
        xsend[t] = x_ref[rows(f), t * k:(t + 1) * k]
    pl.semaphore_wait(barrier, len(greeted))
    for d in range(n - 1, 0, -1):
        for sign in (1, -1):
            t = z + sign * d
            send(
                (t < n) & (t >= 0),
                lambda t=t, d=d, sign=sign: copy(
                    xsend.at[t], xall.at[f, rows(z)], x1_s.at[t], x1_r.at[z], (layer, f, t)
                ),
            )
    for t in range(n):
        @pl.when(t == z)
        def _(t=t):
            for p in range(n):
                xall[p, t * r:(t + 1) * r] = x_ref[p * r:(p + 1) * r, t * k:(t + 1) * k]
    load_cross.wait()
    send(second, lambda: copy(cross_ref, cross2_ref, cw_s.at[0], cw_r.at[0], (0, f, z)))
    for d in range(1, n):
        for sign in (1, -1):
            t = z + sign * d
            ok = (t < n) & (t >= 0)

            def wait(t=t):
                arrive(None, xall.at[f, rows(t)], x1_r.at[t])
            pl.when(ok)(wait)
            for dx in range(1, n):
                send(
                    ok,
                    lambda t=t, dx=dx: copy(
                        xall.at[f, rows(t)], xall.at[f, rows(t)],
                        x2_s.at[dx, t], x2_r.at[dx, t], (layer, peer(dx), z)
                    ),
                )

    per_piece = ROW_CUTS * COL_CUTS
    steps = n * per_piece
    ru, wide = r // ROW_CUTS, enc_ref.shape[1] // COL_CUTS
    _, ahead, lists = plan_line(n, steps, per_piece)

    def where(s, t):
        i, rest = s // per_piece, s % per_piece
        u, c = rest // COL_CUTS, rest % COL_CUTS
        return i, slice(t * r + u * ru, t * r + (u + 1) * ru), slice(c * wide, (c + 1) * wide)

    def view(ref, s, t):
        i, part, cols = where(s, t)
        return ref.at[i, pl.ds(part.start, ru), pl.ds(cols.start, wide)]

    later = {}

    def go(zz, make):
        make().start()
        later.setdefault(zz, []).append(make)

    def pass_sum(zz, s, t, way):
        buf, sem = (rs_up, ru_r) if way > 0 else (rs_dn, rd_r)
        go(zz, lambda: copy(
            view(rs_send, s, t), view(buf, s, t), rs_s.at[s, t], sem.at[s, t], (layer, f, zz + way)))

    def pass_features(zz, s, t, way):
        ss, rr = (au_s, au_r) if way > 0 else (ad_s, ad_r)
        go(zz, lambda: copy(
            view(feats, s, t), view(feats, s, t), ss.at[s, t], rr.at[s, t], (layer, f, zz + way)))

    def handle(zz, event):
        kind, s, t, way = event
        if kind == "init":
            for t in range(n - 1, 0, -1) if zz == 0 else range(n - 1):
                pass_sum(zz, s, t, 1 if zz == 0 else -1)
        elif kind == "relay":
            buf, sem = (rs_up, ru_r) if way > 0 else (rs_dn, rd_r)
            arrive(None, view(buf, s, t), sem.at[s, t])
            at = where(s, t)
            rs_send[at] = (pf[at] + buf[at].astype(F32)).astype(BF16)
            pass_sum(zz, s, t, way)
        elif kind == "own":
            at = where(s, zz)
            total = pf[at] + encb_ref[:, at[2]]
            if zz > 0:
                arrive(None, view(rs_up, s, zz), ru_r.at[s, zz])
                total += rs_up[at].astype(F32)
            if zz < n - 1:
                arrive(None, view(rs_dn, s, zz), rd_r.at[s, zz])
                total += rs_dn[at].astype(F32)
            feats[at] = jnp.maximum(total, 0.0).astype(BF16)
            for way in (1, -1):
                if 0 <= zz + way < n:
                    pass_features(zz, s, zz, way)
        else:
            arrive(None, view(feats, s, t), (au_r if way > 0 else ad_r).at[s, t])
            if 0 <= zz + way < n:
                pass_features(zz, s, t, way)

    def stage_a(i):
        dx = order[i]
        p = peer(dx)
        if dx:
            for t in range(n):
                arrive(t != z, xall.at[p, rows(t)], x2_r.at[n - dx, t])
        pf[i] = jnp.dot(xall[p], enc_ref[...], preferred_element_type=F32)

        @pl.when((z == 0) | (z == n - 1))
        def _():
            rs_send[i] = pf[i].astype(BF16)

    def stage_d(i):
        dx = order[i]
        terms = jnp.dot(feats[i], dec_ref[...], preferred_element_type=F32)
        if dx:
            osend[dx] = terms.astype(BF16)
            send(None, lambda: copy(
                osend.at[dx], orecv.at[dx], o_s.at[dx], o_r.at[dx], (layer, peer(dx), z)))
        else:
            oown[...] = terms

        @pl.when(first)
        def _():
            a = jnp.dot(feats[i], cross_ref[...], preferred_element_type=F32)
            b = jnp.dot(feats[i], cross2_ref[...], preferred_element_type=F32)
            csend[dx] = jnp.concatenate([a, b], axis=1).astype(BF16)
        send(first, lambda: copy(
            csend.at[dx], crecv.at[dx], c_s.at[dx], c_r.at[dx], (1, peer(dx), z)))

    stage_a(0)
    early = min(ahead, per_piece)
    for zz in (0, n - 1):
        @pl.when(z == zz)
        def _(zz=zz):
            for s in range(early):
                handle(zz, ("init", s, 0, 0))
    for i in range(1, n):
        stage_a(i)
    load_dec.wait()
    arrive(first, cross2_ref, cw_r.at[0])
    segments = []
    for zz in range(n):
        parts = [[]]
        for event in lists[zz]:
            if event[0] == "piece":
                parts.append([])
            elif event[0] != "init" or event[1] >= early:
                parts[-1].append(event)
        segments.append(parts)
    for i in range(n):
        for zz in range(n):
            @pl.when(z == zz)
            def _(zz=zz, i=i):
                for event in segments[zz][i]:
                    handle(zz, event)
        stage_d(i)

    for dx in range(1, n):
        arrive(None, orecv.at[dx], o_r.at[dx])
        oown[...] += orecv[dx].astype(F32)
    for t in range(n):
        rsum[t] = oown[t * r:(t + 1) * r].astype(BF16)

    def scatter(cond, src, dst, ss, rs, t):
        send(cond, lambda: copy(src.at[t], dst.at[z], ss.at[t], rs.at[z], (layer, f, t)))

    for t in range(n):
        scatter(t != z, rsum, ztr, e_s, e_r, t)
    for dx in range(n):
        arrive(second, crecv.at[dx], c_r.at[dx])

    @pl.when(second)
    def _():
        sums = crecv[0].astype(F32)
        for dx in range(1, n):
            sums += crecv[dx].astype(F32)
        for t in range(n):
            for h in range(2):
                crs[h, t] = sums[t * r:(t + 1) * r, h * half:(h + 1) * half].astype(BF16)
    for t in range(n):
        for h in range(2):
            scatter(second & (t != z), crs.at[h], zcr.at[h], ec_s.at[h], ec_r.at[h], t)
    ztr[z] = rsum[z]

    @pl.when(second)
    def _():
        for h in range(2):
            zcr[h, z] = crs[h, z]

    for t in range(n):
        arrive(t != z, ztr.at[t], e_r.at[t])

        @pl.when(t == f)
        def _(t=t):
            fin[f] = ztr[t]
        send(t != f, lambda t=t: copy(
            ztr.at[t], fin.at[f], f_s.at[t], f_r.at[f], (layer, t, z)))
    for t in range(n):
        for h in range(2):
            arrive(second & (t != z), zcr.at[h, t], ec_r.at[h, t])
            to, j = (h * n + t) // 2, (h * n + t) % 2

            @pl.when(second & (to == f))
            def _(t=t, h=h, j=j):
                fcr[j, f] = zcr[h, t]
            send(second & (to != f), lambda t=t, h=h, to=to, j=j: copy(
                zcr.at[h, t], fcr.at[j, f], fc_s.at[h, t], fc_r.at[j, f], (layer, to, z)))
    for g in range(n):
        arrive(g != f, fin.at[g], f_r.at[g])
        for j in range(2):
            arrive(second & (g != f), fcr.at[j, g], fc_r.at[j, g])
        part = slice(g * r, (g + 1) * r)

        @pl.when(first)
        def _(g=g, part=part):
            out_ref[part] = (fin[g].astype(F32) + decb_ref[...]).astype(BF16)

        @pl.when(second)
        def _(g=g, part=part):
            cross = jnp.concatenate([fcr[0, g].astype(F32), fcr[1, g].astype(F32)], axis=1)
            out_ref[part] = (fin[g].astype(F32) + cross + decb_ref[...]).astype(BF16)

    for zz in range(n):
        @pl.when(z == zz)
        def _(zz=zz):
            for make in later[zz]:
                make().wait_send()
    for cond, make in pending:
        if cond is None:
            make().wait_send()
        else:
            pl.when(cond)(lambda make=make: make().wait_send())


def by_kernel(n, mlp_inputs, enc_weight, enc_bias, dec_weight, dec_cross, dec_bias):
    x, enc, dec = mlp_inputs[0], enc_weight[0], dec_weight[0]
    r = x.shape[0] // n
    k, wide = enc.shape
    cols, half = dec.shape[1], dec_cross.shape[1]
    vmem = pl.BlockSpec(memory_space=pltpu.VMEM)
    hbm = pl.BlockSpec(memory_space=pl.ANY)
    dma = pltpu.SemaphoreType.DMA
    every, steps = n * r, n * ROW_CUTS * COL_CUTS
    scratch = [
        pltpu.VMEM(dec.shape, BF16),
        pltpu.VMEM(dec_cross.shape, BF16),
        pltpu.VMEM(dec_cross.shape, BF16),
        pltpu.VMEM((n, r, k), BF16),
        pltpu.VMEM((n, every, k), BF16),
        pltpu.VMEM((n, every, wide), F32),
        pltpu.VMEM((n, every, wide), BF16),
        pltpu.VMEM((n, every, wide), BF16),
        pltpu.VMEM((n, every, wide), BF16),
        pltpu.VMEM((n, every, wide), BF16),
        pltpu.VMEM((every, cols), F32),
        pltpu.VMEM((n, every, cols), BF16),
        pltpu.VMEM((n, every, cols), BF16),
        pltpu.VMEM((n, every, 2 * half), BF16),
        pltpu.VMEM((n, every, 2 * half), BF16),
        pltpu.VMEM((n, r, cols), BF16),
        pltpu.VMEM((n, r, cols), BF16),
        pltpu.VMEM((2, n, r, half), BF16),
        pltpu.VMEM((2, n, r, half), BF16),
        pltpu.VMEM((n, r, cols), BF16),
        pltpu.VMEM((2, n, r, half), BF16),
        dma((2,)), dma((1,)), dma((1,)),
        dma((n,)), dma((n,)), dma((n, n)), dma((n, n)),
        dma((steps, n)), dma((steps, n)), dma((steps, n)),
        dma((steps, n)), dma((steps, n)), dma((steps, n)), dma((steps, n)),
        dma((n,)), dma((n,)), dma((n,)), dma((n,)),
        dma((n,)), dma((n,)), dma((2, n)), dma((2, n)),
        dma((n,)), dma((n,)), dma((2, n)), dma((2, n)),
    ]
    out = pl.pallas_call(
        functools.partial(kernel, n),
        out_shape=jax.ShapeDtypeStruct((x.shape[0], cols), BF16),
        in_specs=[vmem, vmem, vmem, hbm, hbm, vmem],
        out_specs=vmem,
        scratch_shapes=scratch,
        compiler_params=pltpu.CompilerParams(
            collective_id=0, has_side_effects=True, vmem_limit_bytes=56 * 2**20
        ),
    )(x, enc, enc_bias, dec, dec_cross, dec_bias)
    return out[None]


def solution(mesh):
    placed = (
        P("layer", "seq", None),
        P("layer", "seq", "feat"),
        P("layer", "feat"),
        P("layer", "feat", "seq"),
        P("feat", ("layer", "seq")),
        P("layer", "feat"),
    )
    groups = mesh.shape["feat"]

    def body(mlp_inputs, *rest):
        fits = groups == mesh.shape["seq"] and mlp_inputs.shape[1] % (16 * ROW_CUTS * groups) == 0
        if fits and mesh.shape["layer"] == 2 and groups % 2 == 0:
            return by_kernel(groups, mlp_inputs, *rest)
        return per_device(mlp_inputs, *rest)

    return jax.shard_map(
        body, mesh=mesh, in_specs=placed, out_specs=P("layer", "seq", "feat"), check_vma=False
    )
```

```python
import functools
import heapq

import jax
import jax.numpy as jnp
from jax import lax
from jax.experimental import pallas as pl
from jax.experimental.pallas import tpu as pltpu
from jax.sharding import PartitionSpec as P

MESH = pl.DeviceIdType.MESH
F32, BF16 = jnp.float32, jnp.bfloat16


def passed_along(x, axis, by):
    devices = lax.axis_size(axis)
    pairs = [(i, i + by) for i in range(devices) if 0 <= i + by < devices]
    return lax.ppermute(x, axis, pairs)


def per_device(mlp_inputs, enc_weight, enc_bias, dec_weight, dec_cross, dec_bias):
    token_rows = mlp_inputs[0]
    layer_index = lax.axis_index("layer")
    pre_acts = jnp.dot(
        token_rows,
        lax.all_gather(enc_weight[0], "seq", axis=0, tiled=True),
        preferred_element_type=F32,
    )
    features = jnp.maximum(pre_acts + enc_bias[0], 0.0).astype(BF16)
    own_terms = jnp.dot(
        features,
        lax.all_gather(dec_weight[0], "seq", axis=1, tiled=True),
        preferred_element_type=F32,
    )
    half_rows = features.shape[0] // 2
    sent_half = passed_along(features[half_rows:], "layer", 1)
    cross_input = jnp.where(layer_index == 0, features[:half_rows], sent_half)
    cross_terms = jnp.dot(
        cross_input,
        lax.all_gather(dec_cross, ("layer", "seq"), axis=1, tiled=True),
        preferred_element_type=F32,
    )
    own_sums, cross_sums = (
        lax.psum_scatter(own_terms, "feat", scatter_dimension=1, tiled=True),
        lax.psum_scatter(cross_terms, "feat", scatter_dimension=1, tiled=True),
    )
    moved_sums = passed_along(cross_sums, "layer", 1)
    cross_full = jnp.concatenate([moved_sums, cross_sums], axis=0)
    total = own_sums + dec_bias[0] + jnp.where(layer_index == 1, cross_full, 0.0)
    return total.astype(BF16)[None]

ROW_CUTS, COL_CUTS = 3, 1


def decoded(features, columns):
    return lax.dot_general(features, columns, (((1,), (1,)), ((), ())), preferred_element_type=F32)


def plan_line(n, steps, per_piece, piece=2.1, lag=1.7, touch=0.1):
    wire = piece / per_piece

    def run(ahead):
        link, free = {}, [0.0] * n
        got, todo, heap, lists = {}, {}, [], [[] for _ in range(n)]
        serial = [0]

        def post(now, z, to, msg):
            start = max(link.get((z, to), 0.0), now)
            link[z, to] = start + wire
            serial[0] += 1
            heapq.heappush(heap, (start + wire + lag, serial[0], to, msg))

        def start(now, z, s):
            if s < steps and z in (0, n - 1):
                lists[z].append(("init", s, 0, 0))
                for t in range(n - 1, 0, -1) if z == 0 else range(n - 1):
                    post(now, z, 1 if z == 0 else n - 2, ("rs", s, t, 1 if z == 0 else -1))

        def finish(z, s):
            key = (z, s // per_piece)
            todo[key] = todo.get(key, 0) + 1
            if todo[key] == per_piece * n:
                lists[z].append(("piece", s // per_piece, 0, 0))

        for s in range(ahead):
            for z in (0, n - 1):
                start(0.0, z, s)
        while heap:
            now, _, z, (kind, s, t, way) = heapq.heappop(heap)
            now = max(now, free[z]) + touch
            free[z] = now
            if kind == "rs" and t != z:
                lists[z].append(("relay", s, t, way))
                post(now, z, z + way, (kind, s, t, way))
            elif kind == "rs":
                got[z, s] = got.get((z, s), 0) + 1
                if got[z, s] == (z > 0) + (z < n - 1):
                    lists[z].append(("own", s, 0, 0))
                    for to in (z + 1, z - 1):
                        if 0 <= to < n:
                            post(now, z, to, ("ag", s, z, to - z))
                    start(now, z, s + ahead)
                    finish(z, s)
            else:
                lists[z].append(("ag", s, t, way))
                if 0 <= z + way < n:
                    post(now, z, z + way, (kind, s, t, way))
                finish(z, s)
        return max(free), ahead, lists

    return min(run(ahead) for ahead in range(1, steps + 1))


def kernel(
    n, x_ref, enc_ref, encb_ref, dec_hbm, cross_hbm, decb_ref, out_ref,
    dec_ref, cross_ref, xsend, xall, pf, rs_send, rs_up, rs_dn, feats,
    oown, osend, orecv, csend, crecv, rsum, ztr, crs, zcr, fin, fcr,
    ld_sem, cw_s, cw_r, x1_s, x1_r, x2_s, x2_r, rs_s, ru_r, rd_r, au_s, au_r, ad_s, ad_r,
    o_s, o_r, c_s, c_r, e_s, e_r, ec_s, ec_r, f_s, f_r, fc_s, fc_r,
):
    layer, f, z = lax.axis_index("layer"), lax.axis_index("feat"), lax.axis_index("seq")
    r = x_ref.shape[0] // n
    k = enc_ref.shape[0]
    half = cross_hbm.shape[0]
    near, far = pl.ds(0, half), pl.ds(half, half)
    first, second = layer == 0, layer == 1
    order = list(range(1, n)) + [0]

    def peer(dx):
        return lax.rem(f + dx, n)

    def rows(t):
        return pl.ds(pl.multiple_of(t * r, r), r)

    pending = []

    def copy(src, dst, ss, rs, to):
        a, b, c = to
        return pltpu.make_async_remote_copy(
            src_ref=src, dst_ref=dst, send_sem=ss, recv_sem=rs,
            device_id={"layer": a, "feat": b, "seq": c}, device_id_type=MESH,
        )

    def send(cond, make):
        if cond is None:
            make().start()
        else:
            pl.when(cond)(lambda: make().start())
        pending.append((cond, make))

    def arrive(cond, dst, sem):
        def wait():
            copy(dst, dst, sem, sem, (layer, f, z)).wait_recv()
        if cond is None:
            wait()
        else:
            pl.when(cond)(wait)

    load_dec = pltpu.make_async_copy(dec_hbm, dec_ref, ld_sem.at[0])
    load_dec.start()
    load_cross = pltpu.make_async_copy(cross_hbm, cross_ref.at[near], ld_sem.at[1])
    load_cross.start()

    barrier = pltpu.get_barrier_semaphore()
    greeted = [(layer, f, lax.rem(z + d, n)) for d in range(1, n)]
    greeted += [(layer, peer(d), z) for d in range(1, n)]
    greeted += [(1 - layer, peer(d), z) for d in range(n)]
    for a, b, c in greeted:
        pl.semaphore_signal(
            barrier, inc=1, device_id={"layer": a, "feat": b, "seq": c}, device_id_type=MESH
        )

    for t in range(n):
        xsend[t] = x_ref[rows(f), t * k:(t + 1) * k]
    pl.semaphore_wait(barrier, len(greeted))
    for d in range(n - 1, 0, -1):
        for sign in (1, -1):
            t = z + sign * d
            send(
                (t < n) & (t >= 0),
                lambda t=t, d=d, sign=sign: copy(
                    xsend.at[t], xall.at[f, rows(z)], x1_s.at[t], x1_r.at[z], (layer, f, t)
                ),
            )
    for t in range(n):
        @pl.when(t == z)
        def _(t=t):
            for p in range(n):
                xall[p, t * r:(t + 1) * r] = x_ref[p * r:(p + 1) * r, t * k:(t + 1) * k]
    load_cross.wait()
    send(second, lambda: copy(
        cross_ref.at[near], cross_ref.at[far], cw_s.at[0], cw_r.at[0], (0, f, z)))
    def forward(dx, t, ok):
        send(ok, lambda: copy(
            xall.at[f, rows(t)], xall.at[f, rows(t)],
            x2_s.at[dx, t], x2_r.at[dx, t], (layer, peer(dx), z)))

    for d in range(1, n):
        for sign in (1, -1):
            t = z + sign * d
            ok = (t < n) & (t >= 0)

            def wait(t=t):
                arrive(None, xall.at[f, rows(t)], x1_r.at[t])
            pl.when(ok)(wait)
            forward(n - 1, t, ok)
    for dx in range(n - 2, 0, -1):
        for t in range(n):
            forward(dx, t, t != z)

    per_piece = ROW_CUTS * COL_CUTS
    steps = n * per_piece
    ru, wide = r // ROW_CUTS, enc_ref.shape[1] // COL_CUTS
    _, ahead, lists = plan_line(n, steps, per_piece)

    def where(s, t):
        i, rest = s // per_piece, s % per_piece
        u, c = rest // COL_CUTS, rest % COL_CUTS
        return i, slice(t * r + u * ru, t * r + (u + 1) * ru), slice(c * wide, (c + 1) * wide)

    def view(ref, s, t):
        i, part, cols = where(s, t)
        return ref.at[i, pl.ds(part.start, ru), pl.ds(cols.start, wide)]

    later = {}

    def go(zz, make):
        make().start()
        later.setdefault(zz, []).append(make)

    def pass_sum(zz, s, t, way):
        buf, sem = (rs_up, ru_r) if way > 0 else (rs_dn, rd_r)
        go(zz, lambda: copy(
            view(rs_send, s, t), view(buf, s, t), rs_s.at[s, t], sem.at[s, t], (layer, f, zz + way)))

    def pass_features(zz, s, t, way):
        ss, rr = (au_s, au_r) if way > 0 else (ad_s, ad_r)
        go(zz, lambda: copy(
            view(feats, s, t), view(feats, s, t), ss.at[s, t], rr.at[s, t], (layer, f, zz + way)))

    def handle(zz, event):
        kind, s, t, way = event
        if kind == "init":
            for t in range(n - 1, 0, -1) if zz == 0 else range(n - 1):
                pass_sum(zz, s, t, 1 if zz == 0 else -1)
        elif kind == "relay":
            buf, sem = (rs_up, ru_r) if way > 0 else (rs_dn, rd_r)
            arrive(None, view(buf, s, t), sem.at[s, t])
            at = where(s, t)
            rs_send[at] = (pf[at] + buf[at].astype(F32)).astype(BF16)
            pass_sum(zz, s, t, way)
        elif kind == "own":
            at = where(s, zz)
            total = pf[at] + encb_ref[:, at[2]]
            if zz > 0:
                arrive(None, view(rs_up, s, zz), ru_r.at[s, zz])
                total += rs_up[at].astype(F32)
            if zz < n - 1:
                arrive(None, view(rs_dn, s, zz), rd_r.at[s, zz])
                total += rs_dn[at].astype(F32)
            feats[at] = jnp.maximum(total, 0.0).astype(BF16)
            for way in (1, -1):
                if 0 <= zz + way < n:
                    pass_features(zz, s, zz, way)
        else:
            arrive(None, view(feats, s, t), (au_r if way > 0 else ad_r).at[s, t])
            if 0 <= zz + way < n:
                pass_features(zz, s, t, way)

    def stage_a(i):
        dx = order[i]
        p = peer(dx)
        if dx:
            for t in range(n):
                arrive(t != z, xall.at[p, rows(t)], x2_r.at[n - dx, t])
        pf[i] = jnp.dot(xall[p], enc_ref[...], preferred_element_type=F32)

        @pl.when((z == 0) | (z == n - 1))
        def _():
            rs_send[i] = pf[i].astype(BF16)

    def stage_d(i):
        dx = order[i]
        terms = decoded(feats[i], dec_ref[...])
        if dx:
            osend[dx] = terms.astype(BF16)
            send(None, lambda: copy(
                osend.at[dx], orecv.at[dx], o_s.at[dx], o_r.at[dx], (layer, peer(dx), z)))
        else:
            oown[...] = terms

        @pl.when(first)
        def _():
            csend[dx] = decoded(feats[i], cross_ref[...]).astype(BF16)
        send(first, lambda: copy(
            csend.at[dx], crecv.at[dx], c_s.at[dx], c_r.at[dx], (1, peer(dx), z)))

    stage_a(0)
    early = min(ahead, per_piece)
    for zz in (0, n - 1):
        @pl.when(z == zz)
        def _(zz=zz):
            for s in range(early):
                handle(zz, ("init", s, 0, 0))
    for i in range(1, n):
        stage_a(i)
    load_dec.wait()
    arrive(first, cross_ref.at[far], cw_r.at[0])
    segments = []
    for zz in range(n):
        parts = [[]]
        for event in lists[zz]:
            if event[0] == "piece":
                parts.append([])
            elif event[0] != "init" or event[1] >= early:
                parts[-1].append(event)
        segments.append(parts)
    for i in range(n):
        for zz in range(n):
            @pl.when(z == zz)
            def _(zz=zz, i=i):
                for event in segments[zz][i]:
                    handle(zz, event)
        stage_d(i)

    for dx in range(1, n):
        arrive(None, orecv.at[dx], o_r.at[dx])
        oown[...] += orecv[dx].astype(F32)
    for t in range(n):
        rsum[t] = oown[t * r:(t + 1) * r].astype(BF16)

    def scatter(cond, src, dst, ss, rs, t):
        send(cond, lambda: copy(src.at[t], dst.at[z], ss.at[t], rs.at[z], (layer, f, t)))

    for t in range(n):
        scatter(t != z, rsum, ztr, e_s, e_r, t)
    for dx in range(n):
        arrive(second, crecv.at[dx], c_r.at[dx])

    @pl.when(second)
    def _():
        sums = crecv[0].astype(F32)
        for dx in range(1, n):
            sums += crecv[dx].astype(F32)
        for t in range(n):
            for h in range(2):
                crs[h, t] = sums[t * r:(t + 1) * r, h * half:(h + 1) * half].astype(BF16)
    for t in range(n):
        for h in range(2):
            scatter(second & (t != z), crs.at[h], zcr.at[h], ec_s.at[h], ec_r.at[h], t)
    ztr[z] = rsum[z]

    @pl.when(second)
    def _():
        for h in range(2):
            zcr[h, z] = crs[h, z]

    for t in range(n):
        arrive(t != z, ztr.at[t], e_r.at[t])

        @pl.when(t == f)
        def _(t=t):
            fin[f] = ztr[t]
        send(t != f, lambda t=t: copy(
            ztr.at[t], fin.at[f], f_s.at[t], f_r.at[f], (layer, t, z)))
    for t in range(n):
        for h in range(2):
            arrive(second & (t != z), zcr.at[h, t], ec_r.at[h, t])
            to, j = (h * n + t) // 2, (h * n + t) % 2

            @pl.when(second & (to == f))
            def _(t=t, h=h, j=j):
                fcr[j, f] = zcr[h, t]
            send(second & (to != f), lambda t=t, h=h, to=to, j=j: copy(
                zcr.at[h, t], fcr.at[j, f], fc_s.at[h, t], fc_r.at[j, f], (layer, to, z)))
    for g in range(n):
        arrive(g != f, fin.at[g], f_r.at[g])
        for j in range(2):
            arrive(second & (g != f), fcr.at[j, g], fc_r.at[j, g])
        part = slice(g * r, (g + 1) * r)

        @pl.when(first)
        def _(g=g, part=part):
            out_ref[part] = (fin[g].astype(F32) + decb_ref[...]).astype(BF16)

        @pl.when(second)
        def _(g=g, part=part):
            cross = jnp.concatenate([fcr[0, g].astype(F32), fcr[1, g].astype(F32)], axis=1)
            out_ref[part] = (fin[g].astype(F32) + cross + decb_ref[...]).astype(BF16)

    for zz in range(n):
        @pl.when(z == zz)
        def _(zz=zz):
            for make in later[zz]:
                make().wait_send()
    for cond, make in pending:
        if cond is None:
            make().wait_send()
        else:
            pl.when(cond)(lambda make=make: make().wait_send())


def by_kernel(n, mlp_inputs, enc_weight, enc_bias, dec_weight, dec_cross, dec_bias):
    x, enc, dec, cross = mlp_inputs[0], enc_weight[0], dec_weight[0].T, dec_cross.T
    r = x.shape[0] // n
    k, wide = enc.shape
    cols, half = dec.shape[0], cross.shape[0]
    vmem = pl.BlockSpec(memory_space=pltpu.VMEM)
    hbm = pl.BlockSpec(memory_space=pl.ANY)
    dma = pltpu.SemaphoreType.DMA
    every, steps = n * r, n * ROW_CUTS * COL_CUTS
    scratch = [
        pltpu.VMEM(dec.shape, BF16),
        pltpu.VMEM((2 * half, cross.shape[1]), BF16),
        pltpu.VMEM((n, r, k), BF16),
        pltpu.VMEM((n, every, k), BF16),
        pltpu.VMEM((n, every, wide), F32),
        pltpu.VMEM((n, every, wide), BF16),
        pltpu.VMEM((n, every, wide), BF16),
        pltpu.VMEM((n, every, wide), BF16),
        pltpu.VMEM((n, every, wide), BF16),
        pltpu.VMEM((every, cols), F32),
        pltpu.VMEM((n, every, cols), BF16),
        pltpu.VMEM((n, every, cols), BF16),
        pltpu.VMEM((n, every, 2 * half), BF16),
        pltpu.VMEM((n, every, 2 * half), BF16),
        pltpu.VMEM((n, r, cols), BF16),
        pltpu.VMEM((n, r, cols), BF16),
        pltpu.VMEM((2, n, r, half), BF16),
        pltpu.VMEM((2, n, r, half), BF16),
        pltpu.VMEM((n, r, cols), BF16),
        pltpu.VMEM((2, n, r, half), BF16),
        dma((2,)), dma((1,)), dma((1,)),
        dma((n,)), dma((n,)), dma((n, n)), dma((n, n)),
        dma((steps, n)), dma((steps, n)), dma((steps, n)),
        dma((steps, n)), dma((steps, n)), dma((steps, n)), dma((steps, n)),
        dma((n,)), dma((n,)), dma((n,)), dma((n,)),
        dma((n,)), dma((n,)), dma((2, n)), dma((2, n)),
        dma((n,)), dma((n,)), dma((2, n)), dma((2, n)),
    ]
    out = pl.pallas_call(
        functools.partial(kernel, n),
        out_shape=jax.ShapeDtypeStruct((x.shape[0], cols), BF16),
        in_specs=[vmem, vmem, vmem, hbm, hbm, vmem],
        out_specs=vmem,
        scratch_shapes=scratch,
        compiler_params=pltpu.CompilerParams(
            collective_id=0, has_side_effects=True, vmem_limit_bytes=56 * 2**20
        ),
    )(x, enc, enc_bias, dec, cross, dec_bias)
    return out[None]


def solution(mesh):
    placed = (
        P("layer", "seq", None),
        P("layer", "seq", "feat"),
        P("layer", "feat"),
        P("layer", "feat", "seq"),
        P("feat", ("layer", "seq")),
        P("layer", "feat"),
    )
    groups = mesh.shape["feat"]

    def body(mlp_inputs, *rest):
        fits = groups == mesh.shape["seq"] and mlp_inputs.shape[1] % (16 * ROW_CUTS * groups) == 0
        if fits and mesh.shape["layer"] == 2 and groups % 2 == 0:
            return by_kernel(groups, mlp_inputs, *rest)
        return per_device(mlp_inputs, *rest)

    return jax.shard_map(
        body, mesh=mesh, in_specs=placed, out_specs=P("layer", "seq", "feat"), check_vma=False
    )
```

```python
import functools
import heapq

import jax
import jax.numpy as jnp
from jax import lax
from jax.experimental import pallas as pl
from jax.experimental.pallas import tpu as pltpu
from jax.sharding import PartitionSpec as P

MESH = pl.DeviceIdType.MESH
F32, BF16 = jnp.float32, jnp.bfloat16


def passed_along(x, axis, by):
    devices = lax.axis_size(axis)
    pairs = [(i, i + by) for i in range(devices) if 0 <= i + by < devices]
    return lax.ppermute(x, axis, pairs)


def per_device(mlp_inputs, enc_weight, enc_bias, dec_weight, dec_cross, dec_bias):
    token_rows = mlp_inputs[0]
    layer_index = lax.axis_index("layer")
    pre_acts = jnp.dot(
        token_rows,
        lax.all_gather(enc_weight[0], "seq", axis=0, tiled=True),
        preferred_element_type=F32,
    )
    features = jnp.maximum(pre_acts + enc_bias[0], 0.0).astype(BF16)
    own_terms = jnp.dot(
        features,
        lax.all_gather(dec_weight[0], "seq", axis=1, tiled=True),
        preferred_element_type=F32,
    )
    half_rows = features.shape[0] // 2
    sent_half = passed_along(features[half_rows:], "layer", 1)
    cross_input = jnp.where(layer_index == 0, features[:half_rows], sent_half)
    cross_terms = jnp.dot(
        cross_input,
        lax.all_gather(dec_cross, ("layer", "seq"), axis=1, tiled=True),
        preferred_element_type=F32,
    )
    own_sums, cross_sums = (
        lax.psum_scatter(own_terms, "feat", scatter_dimension=1, tiled=True),
        lax.psum_scatter(cross_terms, "feat", scatter_dimension=1, tiled=True),
    )
    moved_sums = passed_along(cross_sums, "layer", 1)
    cross_full = jnp.concatenate([moved_sums, cross_sums], axis=0)
    total = own_sums + dec_bias[0] + jnp.where(layer_index == 1, cross_full, 0.0)
    return total.astype(BF16)[None]

ROW_CUTS, COL_CUTS = 3, 1


def decoded(features, columns):
    return lax.dot_general(features, columns, (((1,), (1,)), ((), ())), preferred_element_type=F32)


def plan_line(n, steps, per_piece, piece=2.1, lag=1.7, touch=0.1):
    wire = piece / per_piece

    def run(ahead):
        link, free = {}, [0.0] * n
        got, todo, heap, lists = {}, {}, [], [[] for _ in range(n)]
        serial = [0]

        def post(now, z, to, msg):
            start = max(link.get((z, to), 0.0), now)
            link[z, to] = start + wire
            serial[0] += 1
            heapq.heappush(heap, (start + wire + lag, serial[0], to, msg))

        def start(now, z, s):
            if s < steps and z in (0, n - 1):
                lists[z].append(("init", s, 0, 0))
                for t in range(n - 1, 0, -1) if z == 0 else range(n - 1):
                    post(now, z, 1 if z == 0 else n - 2, ("rs", s, t, 1 if z == 0 else -1))

        def finish(z, s):
            key = (z, s // per_piece)
            todo[key] = todo.get(key, 0) + 1
            if todo[key] == per_piece * n:
                lists[z].append(("piece", s // per_piece, 0, 0))

        for s in range(ahead):
            for z in (0, n - 1):
                start(0.0, z, s)
        while heap:
            now, _, z, (kind, s, t, way) = heapq.heappop(heap)
            now = max(now, free[z]) + touch
            free[z] = now
            if kind == "rs" and t != z:
                lists[z].append(("relay", s, t, way))
                post(now, z, z + way, (kind, s, t, way))
            elif kind == "rs":
                got[z, s] = got.get((z, s), 0) + 1
                if got[z, s] == (z > 0) + (z < n - 1):
                    lists[z].append(("own", s, 0, 0))
                    for to in (z + 1, z - 1):
                        if 0 <= to < n:
                            post(now, z, to, ("ag", s, z, to - z))
                    start(now, z, s + ahead)
                    finish(z, s)
            else:
                lists[z].append(("ag", s, t, way))
                if 0 <= z + way < n:
                    post(now, z, z + way, (kind, s, t, way))
                finish(z, s)
        return max(free), ahead, lists

    return min(run(ahead) for ahead in range(1, steps + 1))


def kernel(
    n, x_ref, enc_ref, encb_ref, dec_hbm, cross_hbm, decb_ref, out_ref,
    dec_ref, cross_ref, xsend, xall, pf, rs_send, rs_up, rs_dn, feats,
    oown, osend, orecv, csend, crecv, rsum, ztr, crs, zcr, fin, fcr,
    ld_sem, cw_s, cw_r, x1_s, x1_r, x2_s, x2_r, rs_s, ru_r, rd_r, au_s, au_r, ad_s, ad_r,
    o_s, o_r, c_s, c_r, e_s, e_r, ec_s, ec_r, f_s, f_r, fc_s, fc_r,
):
    layer, f, z = lax.axis_index("layer"), lax.axis_index("feat"), lax.axis_index("seq")
    r = x_ref.shape[0] // n
    k = enc_ref.shape[0]
    half = cross_hbm.shape[0]
    near, far = pl.ds(0, half), pl.ds(half, half)
    first, second = layer == 0, layer == 1
    order = list(range(1, n)) + [0]

    def peer(dx):
        return lax.rem(f + dx, n)

    def rows(t):
        return pl.ds(pl.multiple_of(t * r, r), r)

    pending = []

    def copy(src, dst, ss, rs, to):
        a, b, c = to
        return pltpu.make_async_remote_copy(
            src_ref=src, dst_ref=dst, send_sem=ss, recv_sem=rs,
            device_id={"layer": a, "feat": b, "seq": c}, device_id_type=MESH,
        )

    def send(cond, make):
        if cond is None:
            make().start()
        else:
            pl.when(cond)(lambda: make().start())
        pending.append((cond, make))

    def arrive(cond, dst, sem):
        def wait():
            copy(dst, dst, sem, sem, (layer, f, z)).wait_recv()
        if cond is None:
            wait()
        else:
            pl.when(cond)(wait)

    load_dec = pltpu.make_async_copy(dec_hbm, dec_ref, ld_sem.at[0])
    load_dec.start()
    load_cross = pltpu.make_async_copy(cross_hbm, cross_ref.at[near], ld_sem.at[1])
    load_cross.start()

    barrier = pltpu.get_barrier_semaphore()
    greeted = [(layer, f, lax.rem(z + d, n)) for d in range(1, n)]
    greeted += [(layer, peer(d), z) for d in range(1, n)]
    greeted += [(1 - layer, peer(d), z) for d in range(n)]
    for a, b, c in greeted:
        pl.semaphore_signal(
            barrier, inc=1, device_id={"layer": a, "feat": b, "seq": c}, device_id_type=MESH
        )

    for t in range(n):
        xsend[t] = x_ref[rows(f), t * k:(t + 1) * k]
    pl.semaphore_wait(barrier, len(greeted))
    for d in range(n - 1, 0, -1):
        for sign in (1, -1):
            t = z + sign * d
            send(
                (t < n) & (t >= 0),
                lambda t=t, d=d, sign=sign: copy(
                    xsend.at[t], xall.at[f, rows(z)], x1_s.at[t], x1_r.at[z], (layer, f, t)
                ),
            )
    for t in range(n):
        @pl.when(t == z)
        def _(t=t):
            for p in range(n):
                xall[p, t * r:(t + 1) * r] = x_ref[p * r:(p + 1) * r, t * k:(t + 1) * k]
    load_cross.wait()
    send(second, lambda: copy(
        cross_ref.at[near], cross_ref.at[far], cw_s.at[0], cw_r.at[0], (0, f, z)))
    def forward(dx, t, ok):
        send(ok, lambda: copy(
            xall.at[f, rows(t)], xall.at[f, rows(t)],
            x2_s.at[dx, t], x2_r.at[dx, t], (layer, peer(dx), z)))

    for d in range(1, n):
        for sign in (1, -1):
            t = z + sign * d
            ok = (t < n) & (t >= 0)

            def wait(t=t):
                arrive(None, xall.at[f, rows(t)], x1_r.at[t])
            pl.when(ok)(wait)
            forward(n - 1, t, ok)
    for dx in range(n - 2, 0, -1):
        for t in range(n):
            forward(dx, t, t != z)

    per_piece = ROW_CUTS * COL_CUTS
    steps = n * per_piece
    ru, wide = r // ROW_CUTS, enc_ref.shape[1] // COL_CUTS
    _, ahead, lists = plan_line(n, steps, per_piece)

    def where(s, t):
        i, rest = s // per_piece, s % per_piece
        u, c = rest // COL_CUTS, rest % COL_CUTS
        return i, slice(t * r + u * ru, t * r + (u + 1) * ru), slice(c * wide, (c + 1) * wide)

    def view(ref, s, t):
        i, part, cols = where(s, t)
        return ref.at[i, pl.ds(part.start, ru), pl.ds(cols.start, wide)]

    later = {}

    def go(zz, make):
        make().start()
        later.setdefault(zz, []).append(make)

    def pass_sum(zz, s, t, way):
        buf, sem = (rs_up, ru_r) if way > 0 else (rs_dn, rd_r)
        go(zz, lambda: copy(
            view(rs_send, s, t), view(buf, s, t), rs_s.at[s, t], sem.at[s, t], (layer, f, zz + way)))

    def pass_features(zz, s, t, way):
        ss, rr = (au_s, au_r) if way > 0 else (ad_s, ad_r)
        go(zz, lambda: copy(
            view(feats, s, t), view(feats, s, t), ss.at[s, t], rr.at[s, t], (layer, f, zz + way)))

    def handle(zz, event):
        kind, s, t, way = event
        if kind == "init":
            for t in range(n - 1, 0, -1) if zz == 0 else range(n - 1):
                pass_sum(zz, s, t, 1 if zz == 0 else -1)
        elif kind == "relay":
            buf, sem = (rs_up, ru_r) if way > 0 else (rs_dn, rd_r)
            arrive(None, view(buf, s, t), sem.at[s, t])
            at = where(s, t)
            rs_send[at] = (pf[at] + buf[at].astype(F32)).astype(BF16)
            pass_sum(zz, s, t, way)
        elif kind == "own":
            at = where(s, zz)
            total = pf[at] + encb_ref[:, at[2]]
            if zz > 0:
                arrive(None, view(rs_up, s, zz), ru_r.at[s, zz])
                total += rs_up[at].astype(F32)
            if zz < n - 1:
                arrive(None, view(rs_dn, s, zz), rd_r.at[s, zz])
                total += rs_dn[at].astype(F32)
            feats[at] = jnp.maximum(total, 0.0).astype(BF16)
            for way in (1, -1):
                if 0 <= zz + way < n:
                    pass_features(zz, s, zz, way)
        else:
            arrive(None, view(feats, s, t), (au_r if way > 0 else ad_r).at[s, t])
            if 0 <= zz + way < n:
                pass_features(zz, s, t, way)

    def lines(events):
        for zz in range(n):
            if events[zz]:
                @pl.when(z == zz)
                def _(zz=zz):
                    for event in events[zz]:
                        handle(zz, event)

    def stage_a(i):
        dx = order[i]
        p = peer(dx)
        if dx:
            for t in range(n):
                arrive(t != z, xall.at[p, rows(t)], x2_r.at[n - dx, t])
        pf[i] = jnp.dot(xall[p], enc_ref[...], preferred_element_type=F32)

        @pl.when((z == 0) | (z == n - 1))
        def _():
            rs_send[i] = pf[i].astype(BF16)

    def stage_d(i):
        dx = order[i]
        terms = decoded(feats[i], dec_ref[...])
        if dx:
            osend[dx] = terms.astype(BF16)
            send(None, lambda: copy(
                osend.at[dx], orecv.at[dx], o_s.at[dx], o_r.at[dx], (layer, peer(dx), z)))
        else:
            oown[...] = terms

    def stage_x(i):
        dx = order[i]

        @pl.when(first)
        def _():
            csend[dx] = decoded(feats[i], cross_ref[...]).astype(BF16)
        send(first, lambda: copy(
            csend.at[dx], crecv.at[dx], c_s.at[dx], c_r.at[dx], (1, peer(dx), z)))

    stage_a(0)
    early = min(ahead, per_piece)
    for zz in (0, n - 1):
        @pl.when(z == zz)
        def _(zz=zz):
            for s in range(early):
                handle(zz, ("init", s, 0, 0))
    for i in range(1, n):
        stage_a(i)
    load_dec.wait()
    arrive(first, cross_ref.at[far], cw_r.at[0])
    segments = []
    for zz in range(n):
        parts = [[]]
        for event in lists[zz]:
            if event[0] == "piece":
                parts.append([])
            elif event[0] != "init" or event[1] >= early:
                parts[-1].append(event)
        segments.append(parts)
    for i in range(n):
        lines([segments[zz][i][:len(segments[zz][i]) // 2 if i else 0] for zz in range(n)])
        if i:
            stage_x(i - 1)
        lines([segments[zz][i][len(segments[zz][i]) // 2 if i else 0:] for zz in range(n)])
        if i < n - 1:
            stage_d(i)
    stage_x(n - 1)
    stage_d(n - 1)

    for dx in range(1, n):
        arrive(None, orecv.at[dx], o_r.at[dx])
        oown[...] += orecv[dx].astype(F32)
    for t in range(n):
        rsum[t] = oown[t * r:(t + 1) * r].astype(BF16)

    def scatter(cond, src, dst, ss, rs, t):
        send(cond, lambda: copy(src.at[t], dst.at[z], ss.at[t], rs.at[z], (layer, f, t)))

    for t in range(n):
        scatter(t != z, rsum, ztr, e_s, e_r, t)
    for dx in range(n):
        arrive(second, crecv.at[dx], c_r.at[dx])

    @pl.when(second)
    def _():
        sums = crecv[0].astype(F32)
        for dx in range(1, n):
            sums += crecv[dx].astype(F32)
        for t in range(n):
            for h in range(2):
                crs[h, t] = sums[t * r:(t + 1) * r, h * half:(h + 1) * half].astype(BF16)
    for t in range(n):
        for h in range(2):
            scatter(second & (t != z), crs.at[h], zcr.at[h], ec_s.at[h], ec_r.at[h], t)
    ztr[z] = rsum[z]

    @pl.when(second)
    def _():
        for h in range(2):
            zcr[h, z] = crs[h, z]

    for t in range(n):
        arrive(t != z, ztr.at[t], e_r.at[t])

        @pl.when(t == f)
        def _(t=t):
            fin[f] = ztr[t]
        send(t != f, lambda t=t: copy(
            ztr.at[t], fin.at[f], f_s.at[t], f_r.at[f], (layer, t, z)))
    for t in range(n):
        for h in range(2):
            arrive(second & (t != z), zcr.at[h, t], ec_r.at[h, t])
            to, j = (h * n + t) // 2, (h * n + t) % 2

            @pl.when(second & (to == f))
            def _(t=t, h=h, j=j):
                fcr[j, f] = zcr[h, t]
            send(second & (to != f), lambda t=t, h=h, to=to, j=j: copy(
                zcr.at[h, t], fcr.at[j, f], fc_s.at[h, t], fc_r.at[j, f], (layer, to, z)))
    for g in range(n):
        arrive(g != f, fin.at[g], f_r.at[g])
        for j in range(2):
            arrive(second & (g != f), fcr.at[j, g], fc_r.at[j, g])
        part = slice(g * r, (g + 1) * r)

        @pl.when(first)
        def _(g=g, part=part):
            out_ref[part] = (fin[g].astype(F32) + decb_ref[...]).astype(BF16)

        @pl.when(second)
        def _(g=g, part=part):
            cross = jnp.concatenate([fcr[0, g].astype(F32), fcr[1, g].astype(F32)], axis=1)
            out_ref[part] = (fin[g].astype(F32) + cross + decb_ref[...]).astype(BF16)

    for zz in range(n):
        @pl.when(z == zz)
        def _(zz=zz):
            for make in later[zz]:
                make().wait_send()
    for cond, make in pending:
        if cond is None:
            make().wait_send()
        else:
            pl.when(cond)(lambda make=make: make().wait_send())


def by_kernel(n, mlp_inputs, enc_weight, enc_bias, dec_weight, dec_cross, dec_bias):
    x, enc, dec, cross = mlp_inputs[0], enc_weight[0], dec_weight[0].T, dec_cross.T
    r = x.shape[0] // n
    k, wide = enc.shape
    cols, half = dec.shape[0], cross.shape[0]
    vmem = pl.BlockSpec(memory_space=pltpu.VMEM)
    hbm = pl.BlockSpec(memory_space=pl.ANY)
    dma = pltpu.SemaphoreType.DMA
    every, steps = n * r, n * ROW_CUTS * COL_CUTS
    scratch = [
        pltpu.VMEM(dec.shape, BF16),
        pltpu.VMEM((2 * half, cross.shape[1]), BF16),
        pltpu.VMEM((n, r, k), BF16),
        pltpu.VMEM((n, every, k), BF16),
        pltpu.VMEM((n, every, wide), F32),
        pltpu.VMEM((n, every, wide), BF16),
        pltpu.VMEM((n, every, wide), BF16),
        pltpu.VMEM((n, every, wide), BF16),
        pltpu.VMEM((n, every, wide), BF16),
        pltpu.VMEM((every, cols), F32),
        pltpu.VMEM((n, every, cols), BF16),
        pltpu.VMEM((n, every, cols), BF16),
        pltpu.VMEM((n, every, 2 * half), BF16),
        pltpu.VMEM((n, every, 2 * half), BF16),
        pltpu.VMEM((n, r, cols), BF16),
        pltpu.VMEM((n, r, cols), BF16),
        pltpu.VMEM((2, n, r, half), BF16),
        pltpu.VMEM((2, n, r, half), BF16),
        pltpu.VMEM((n, r, cols), BF16),
        pltpu.VMEM((2, n, r, half), BF16),
        dma((2,)), dma((1,)), dma((1,)),
        dma((n,)), dma((n,)), dma((n, n)), dma((n, n)),
        dma((steps, n)), dma((steps, n)), dma((steps, n)),
        dma((steps, n)), dma((steps, n)), dma((steps, n)), dma((steps, n)),
        dma((n,)), dma((n,)), dma((n,)), dma((n,)),
        dma((n,)), dma((n,)), dma((2, n)), dma((2, n)),
        dma((n,)), dma((n,)), dma((2, n)), dma((2, n)),
    ]
    out = pl.pallas_call(
        functools.partial(kernel, n),
        out_shape=jax.ShapeDtypeStruct((x.shape[0], cols), BF16),
        in_specs=[vmem, vmem, vmem, hbm, hbm, vmem],
        out_specs=vmem,
        scratch_shapes=scratch,
        compiler_params=pltpu.CompilerParams(
            collective_id=0, has_side_effects=True, vmem_limit_bytes=56 * 2**20
        ),
    )(x, enc, enc_bias, dec, cross, dec_bias)
    return out[None]


def solution(mesh):
    placed = (
        P("layer", "seq", None),
        P("layer", "seq", "feat"),
        P("layer", "feat"),
        P("layer", "feat", "seq"),
        P("feat", ("layer", "seq")),
        P("layer", "feat"),
    )
    groups = mesh.shape["feat"]

    def body(mlp_inputs, *rest):
        fits = groups == mesh.shape["seq"] and mlp_inputs.shape[1] % (16 * ROW_CUTS * groups) == 0
        if fits and mesh.shape["layer"] == 2 and groups % 2 == 0:
            return by_kernel(groups, mlp_inputs, *rest)
        return per_device(mlp_inputs, *rest)

    return jax.shard_map(
        body, mesh=mesh, in_specs=placed, out_specs=P("layer", "seq", "feat"), check_vma=False
    )
```
